32 devices in a mesh: gx: 2 (over x), gy: 4 (over z), gz: 4 (over y, core).
Axes of the slice: x: 2, y: 2, z: 4, core: 2. Of those that a mesh axis runs over, the one named last changes fastest.
Arguments:
- displacement: bfloat16 [3, 8, 128, 64], P(None, 'gx', 'gy', 'gz'), may hold values from -6 to 6
- lift_weight: bfloat16 [27, 64, 3], replicated, may hold values from -1 to 1
- encode_weight: bfloat16 [27, 64, 64], replicated, may hold values from -0.21875 to 0.21875
- downward_weight: bfloat16 [8, 128, 64], replicated, may hold values from -0.375 to 0.375
- middle_first: bfloat16 [27, 128, 128], replicated, may hold values from -0.15625 to 0.15625
- middle_second: bfloat16 [27, 128, 128], replicated, may hold values from -0.15625 to 0.15625
- up_weight: bfloat16 [8, 64, 128], replicated, may hold values from -0.75 to 0.75
- decode_weight: bfloat16 [27, 64, 128], replicated, may hold values from -0.15625 to 0.15625
- head_weight: bfloat16 [3, 64], replicated, may hold values from -1 to 1
Outputs:
- imitated: float32 [3, 8, 128, 64], P(None, 'gx', 'gy', 'gz')
The draws below stay inside these ranges and needn't reach their ends.
All inputs are finite; a program needn't handle non-finite values.
Results may differ from the reference program's by a relative error of at most 0.0055.
Values may be sent and summed in bfloat16 or wider, within the bound.
A program may use at most 64 MiB of HBM per device.

```python
import jax
import jax.numpy as jnp

C1 = 64
C2 = 128
NX = 8
NY = 128
NZ = 64


def levels(stream_key, shape, pieces, low, top_value):
    loudness, own = 1.0, jax.random.fold_in(stream_key, 6)
    for position, parts in pieces:
        steps = jnp.exp(jax.random.uniform(jax.random.fold_in(own, position), (parts,), jnp.float32, low / len(pieces), top_value / len(pieces)))
        loudness = loudness * jnp.repeat(steps, shape[position] // parts).reshape([-1 if axis == position else 1 for axis in range(len(shape))])
    return loudness


def noise(stream_key, shape, scale, bound, shards=(), kind=jnp.bfloat16):
    entries = jax.random.normal(stream_key, shape, jnp.float32) * scale
    if len(shards) > 0:
        entries = levels(stream_key, shape, shards, -0.22, 0.18) * entries
    return jnp.clip(entries, min=-bound, max=bound).astype(kind)


def setup_inputs(seed: int = 0) -> dict:
    streams_of = jax.random.split(jax.random.key(seed), 10)
    return {
        "displacement": noise(streams_of[0], (3, NX, NY, NZ), 1.0, 6.0, ((1, 2), (2, 4), (3, 4))),
        "lift_weight": noise(streams_of[1], (27, C1, 3), (81 // 2) ** -0.5, 1.0),
        "encode_weight": noise(streams_of[2], (27, C1, C1), (27 * C1 // 2) ** -0.5, 0.21875),
        "downward_weight": noise(streams_of[3], (8, C2, C1), (4 * C1) ** -0.5, 0.375),
        "middle_first": noise(streams_of[4], (27, C2, C2), (27 * C2 // 2) ** -0.5, 0.15625),
        "middle_second": noise(streams_of[5], (27, C2, C2), (27 * C2 // 2) ** -0.5, 0.15625),
        "up_weight": noise(streams_of[6], (8, C1, C2), (C2 // 2) ** -0.5, 0.75),
        "decode_weight": noise(streams_of[7], (27, C1, 2 * C1), (27 * C1) ** -0.5, 0.15625),
        "head_weight": noise(streams_of[8], (3, C1), (C1 // 2) ** -0.5, 1.0),
    }


def apply_relu(value):
    return jnp.where(value > 0, value, 0.1 * value)


def conv_periodic(field, weight_tensor):
    padded = jnp.pad(field, ((0, 0), (1, 1), (1, 1), (1, 1)), mode="wrap")
    size_x, size_y, size_z = field.shape[1], field.shape[2], field.shape[3]
    weights32 = weight_tensor.astype(jnp.float32)
    summed = jnp.zeros((weight_tensor.shape[1], size_x, size_y, size_z), jnp.float32)
    for offset in range(27):
        a, b, c = offset // 9, (offset // 3) % 3, offset % 3
        window = padded[:, a:a + size_x, b:b + size_y, c:c + size_z].astype(jnp.float32)
        summed = summed + jnp.einsum("oi,ixyz->oxyz", weights32[offset], window)
    return summed


def reduce_resolution(fine_level, weight_tensor):
    chans, size_x, size_y, size_z = fine_level.shape
    blocks = fine_level.reshape(chans, size_x // 2, 2, size_y // 2, 2, size_z // 2, 2).astype(jnp.float32)
    kernel = weight_tensor.reshape(2, 2, 2, weight_tensor.shape[1], weight_tensor.shape[2]).astype(jnp.float32)
    return jnp.einsum("abcoi,ixaybzc->oxyz", kernel, blocks)


def upsample(coarse_field, weight_tensor):
    chans, size_x, size_y, size_z = coarse_field.shape
    kernel = weight_tensor.reshape(2, 2, 2, weight_tensor.shape[1], weight_tensor.shape[2]).astype(jnp.float32)
    result = jnp.einsum("abcoi,ixyz->oxaybzc", kernel, coarse_field.astype(jnp.float32))
    return result.reshape(weight_tensor.shape[1], 2 * size_x, 2 * size_y, 2 * size_z)


def reference(displacement, lift_weight, encode_weight, downward_weight, middle_first, middle_second, up_weight, decode_weight, head_weight):
    first = apply_relu(conv_periodic(displacement, lift_weight)).astype(jnp.bfloat16)
    skip_link = apply_relu(conv_periodic(first, encode_weight)).astype(jnp.bfloat16)
    coarse_level = apply_relu(reduce_resolution(skip_link, downward_weight)).astype(jnp.bfloat16)
    middle = apply_relu(conv_periodic(coarse_level, middle_first)).astype(jnp.bfloat16)
    deep = apply_relu(conv_periodic(middle, middle_second)).astype(jnp.bfloat16)
    upsampled = apply_relu(upsample(deep, up_weight)).astype(jnp.bfloat16)
    stacked = jnp.concatenate([skip_link, upsampled], axis=0)
    joined = apply_relu(conv_periodic(stacked, decode_weight)).astype(jnp.bfloat16)
    head = jnp.einsum("oi,ixyz->oxyz", head_weight.astype(jnp.float32), joined.astype(jnp.float32))
    return displacement.astype(jnp.float32) + head
```

```python
import functools

import jax
import jax.numpy as jnp
from jax import lax
from jax.experimental import pallas as pl
from jax.experimental.pallas import tpu as pltpu
from jax.sharding import PartitionSpec as P

AXES = ("gx", "gy", "gz")
MESH = pl.DeviceIdType.MESH
NT = (((1,), (1,)), ((), ()))
DIRS = [
    (dx, dy, dz) for dx in (-1, 0, 1) for dy in (-1, 0, 1) for dz in (-1, 0, 1)
    if (dx, dy, dz) != (0, 0, 0)
]
F32, BF16 = jnp.float32, jnp.bfloat16


def padded_by(cells, width):
    for axis, dim in (("gx", 1), ("gy", 2), ("gz", 3)):
        count = lax.axis_size(axis)
        head = lax.slice_in_dim(cells, 0, width, axis=dim)
        tail = lax.slice_in_dim(cells, cells.shape[dim] - width, cells.shape[dim], axis=dim)
        cells = jnp.concatenate(
            [
                lax.ppermute(tail, axis, [(i, (i + 1) % count) for i in range(count)]),
                cells,
                lax.ppermute(head, axis, [((i + 1) % count, i) for i in range(count)]),
            ],
            axis=dim,
        )
    return cells


def leaky(value):
    return jnp.maximum(value, 0.1 * value)


def rounded(value):
    return leaky(value).astype(BF16)


def dot(rows, weight):
    return lax.dot_general(rows, weight, NT, preferred_element_type=F32)


def neighbour(direction):
    return tuple(
        lax.rem(lax.axis_index(axis) + lax.axis_size(axis) + step, lax.axis_size(axis))
        for axis, step in zip(AXES, direction)
    )


def exchange(body, below, above, first, last, sends, recvs, zc):
    size_x, size_y = body.shape[0] - 2, body.shape[1] // zc - 2
    copies = []
    for number, (dx, dy, dz) in enumerate(DIRS):
        def span(step, size, offset):
            if step == 0:
                return (offset, size, 1)
            return (offset + size - 1, 1, 0) if step > 0 else (offset, 1, size + 1)

        if dz == 0:
            sx, nx, tx = span(dx, size_x, 1)
            sy, ny, ty = span(dy, size_y, 1)
            src = body.at[pl.ds(sx, nx), pl.ds(sy * zc, ny * zc)]
            dst = body.at[pl.ds(tx, nx), pl.ds(ty * zc, ny * zc)]
        else:
            sx, nx, tx = span(dx, size_x, 0)
            sy, ny, ty = span(dy, size_y, 0)
            src = (last if dz > 0 else first).at[pl.ds(sx, nx), pl.ds(sy, ny)]
            dst = (below if dz > 0 else above).at[pl.ds(tx, nx), pl.ds(ty, ny)]
        copies.append(
            pltpu.make_async_remote_copy(
                src_ref=src, dst_ref=dst, send_sem=sends.at[number], recv_sem=recvs.at[number],
                device_id=neighbour((dx, dy, dz)), device_id_type=MESH,
            )
        )
    for copy in copies:
        copy.start()
    return copies


def masks(rows, zc):
    row = lax.rem(lax.broadcasted_iota(jnp.int32, (rows, 128), 0), zc)
    return row == 0, row == zc - 1


def half_mask(rows):
    return lax.broadcasted_iota(jnp.int32, (rows, 128), 1) < 64


def spread(edge, zc):
    return jnp.broadcast_to(edge, (edge.shape[0], zc, 128)).reshape(edge.shape[0] * zc, 128)


def shifted(plane, below, above, zc):
    rows = plane.shape[0]
    start, end = masks(rows, zc)
    down = jnp.where(start, below, pltpu.roll(plane, 1, 0))
    up = jnp.where(end, above, pltpu.roll(plane, rows - 1, 0))
    return down, up


def fine_conv(plane, twin, weight, x0, group, size_y, zc):
    summed = None
    pairs = size_y // 2
    for a in range(3):
        parts = []
        for source in (plane, twin):
            halves = [[], []]
            for g in range(group):
                value = source[x0 + g + a, pl.ds(0, (size_y + 2) * zc), :]
                value = value.reshape(pairs + 1, 2, zc, 128)
                halves[0].append(value[:, 0])
                halves[1].append(value[:, 1])
            parts.append(halves)
        for b in range(4):
            cut = [
                jnp.concatenate(
                    [
                        v[b // 2 : b // 2 + pairs].reshape(pairs * zc, 128)
                        for v in halves[b % 2]
                    ],
                    axis=0,
                ).astype(BF16)
                for halves in parts
            ]
            term = dot(jnp.concatenate(cut, axis=1), weight[4 * a + b])
            summed = term if summed is None else summed + term
    return summed


def coarse_conv(body, low, high, weight, zc):
    size_x, rows = body.shape[0] - 2, body.shape[1] - 2 * zc
    summed = None
    for a in range(3):
        for b in range(3):
            lhs = jnp.concatenate(
                [
                    jnp.concatenate(
                        [ref[x + a, pl.ds(b * zc, rows), :] for x in range(size_x)], axis=0
                    ).astype(BF16)
                    for ref in (low, body, high)
                ],
                axis=1,
            )
            tap = 9 * a + 3 * b
            kernel = jnp.concatenate([weight[tap], weight[tap + 1], weight[tap + 2]], axis=1)
            term = dot(lhs, kernel)
            summed = term if summed is None else summed + term
    return summed


def unet(
    sizes,
    rows_ref, lift_ref, encode_hbm, downward_ref, first_hbm, second_hbm, up_ref,
    skip_hbm, wide_hbm, head_ref,
    out_ref,
    chunks, fp, fe, sp, se, up, ue, acc,
    s_below, s_above, s_first, s_last,
    coarse_bufs, middle_bufs, deep_bufs, low, high,
    encode_w, first_w, second_w, skip_w, wide_w,
    load_sems, send_sems, recv_sems,
):
    size_x, size_y, size_z, rows_y = sizes
    zc, yc, xc = size_z // 2, size_y // 2, size_x // 2
    loads = [
        pltpu.make_async_copy(src, dst, load_sems.at[i])
        for i, (src, dst) in enumerate(
            (
                (encode_hbm, encode_w), (first_hbm, first_w), (second_hbm, second_w),
                (skip_hbm, skip_w), (wide_hbm, wide_w),
            )
        )
    ]
    for load in loads:
        load.start()
    barrier = pltpu.get_barrier_semaphore()
    for direction in DIRS:
        pl.semaphore_signal(barrier, inc=1, device_id=neighbour(direction), device_id_type=MESH)

    lhs = rows_ref[...]
    base = lift_ref[...]
    for p in range(zc + 1):
        z_lo, z_hi = (2 * p, 2 * p + 1) if p < zc else (size_z, -1)
        kernel = jnp.concatenate(
            [
                base if z == -1 else pltpu.roll(base, 3 * (z + 1), 1)
                for z in (z_lo, z_hi)
            ],
            axis=0,
        ).astype(BF16)
        chunks[p] = rounded(dot(lhs, kernel)).astype(F32)
    half = half_mask(rows_y)
    for x in range(size_x + 2):
        span = pl.ds(x * rows_y, rows_y)
        for p in range(zc):
            fp[x, pl.ds(p, rows_y, stride=zc), :] = chunks[p, span, :]
            fe[x, pl.ds(p, rows_y, stride=zc), :] = jnp.where(
                half, chunks[p + 1, span, :], chunks[zc if p == 0 else p - 1, span, :]
            )

    c_body, c_below, c_above, c_first, c_last = coarse_bufs
    m_body, m_below, m_above, m_first, m_last = middle_bufs
    d_body, d_below, d_above, d_first, d_last = deep_bufs
    loads[0].wait()

    @pl.loop(0, xc)
    def _(x):
        skip = rounded(fine_conv(fp, fe, encode_w, 2 * x, 2, size_y, zc))
        half_rows = yc * zc
        coarse = None
        for g in range(2):
            part = skip[g * half_rows : (g + 1) * half_rows]
            term = dot(part, downward_ref[g])
            coarse = term if coarse is None else coarse + term
            wide = part.astype(F32)
            plane = jnp.stack(
                [wide[:, :128].reshape(yc, zc, 128), wide[:, 128:].reshape(yc, zc, 128)], axis=1
            ).reshape(size_y, zc, 128)
            sp[2 * x + g + 1, pl.ds(zc, size_y * zc), :] = plane.reshape(size_y * zc, 128)
            s_first[2 * x + g] = plane[:, 0:1, :]
            s_last[2 * x + g] = plane[:, zc - 1 : zc, :]
        coarse = rounded(coarse).astype(F32)
        c_body[x + 1, pl.ds(zc, half_rows), :] = coarse
        c_first[x] = coarse.reshape(yc, zc, 128)[:, 0:1, :]
        c_last[x] = coarse.reshape(yc, zc, 128)[:, zc - 1 : zc, :]

    pl.semaphore_wait(barrier, len(DIRS))
    coarse_copies = exchange(*coarse_bufs, send_sems.at[0], recv_sems.at[0], zc)
    skip_copies = exchange(
        sp, s_below, s_above, s_first, s_last, send_sems.at[1], recv_sems.at[1], zc
    )

    def coarse_layer(bufs, weight, result):
        body, below, above = bufs[:3]
        for x in range(xc + 2):
            down, upper = shifted(body[x], spread(below[x], zc), spread(above[x], zc), zc)
            low[x] = down
            high[x] = upper
        value = rounded(coarse_conv(body, low, high, weight, zc)).astype(F32)
        target, _, _, first, last = result
        for x in range(xc):
            part = value[x * yc * zc : (x + 1) * yc * zc]
            target[x + 1, pl.ds(zc, yc * zc), :] = part
            first[x] = part.reshape(yc, zc, 128)[:, 0:1, :]
            last[x] = part.reshape(yc, zc, 128)[:, zc - 1 : zc, :]

    for copy in coarse_copies:
        copy.wait_recv()
    loads[1].wait()
    coarse_layer(coarse_bufs, first_w, middle_bufs)
    middle_copies = exchange(*middle_bufs, send_sems.at[2], recv_sems.at[2], zc)

    for copy in middle_copies:
        copy.wait_recv()
    loads[2].wait()
    coarse_layer(middle_bufs, second_w, deep_bufs)
    deep_copies = exchange(*deep_bufs, send_sems.at[3], recv_sems.at[3], zc)

    for copy in skip_copies:
        copy.wait_recv()
    fine_half = half_mask((size_y + 2) * zc)

    @pl.loop(0, size_x + 2)
    def _(x):
        down, upper = shifted(sp[x], spread(s_below[x], zc), spread(s_above[x], zc), zc)
        se[x] = jnp.where(fine_half, upper, down)

    loads[3].wait()

    @pl.loop(0, xc)
    def _(x):
        acc[x] = fine_conv(sp, se, skip_w, 2 * x, 2, size_y, zc)

    for copy in deep_copies:
        copy.wait_recv()
    coarse_rows = (yc + 2) * zc
    _, coarse_end = masks(coarse_rows, zc)

    def interleaved(value):
        even = value[:, 128:].reshape(yc + 2, zc, 128)[: yc + 1]
        odd = value[:, :128].reshape(yc + 2, zc, 128)[1:]
        return jnp.stack([even, odd], axis=1).reshape((size_y + 2) * zc, 128)

    for x in range(size_x + 2):
        source, a = (x + 1) // 2, (x + 1) % 2
        kernel = jnp.concatenate([up_ref[2 * a], up_ref[2 * a + 1]], axis=0)
        edge_rows = jnp.where(
            coarse_end, spread(d_above[source], zc), spread(d_below[source], zc)
        )
        plane = interleaved(rounded(dot(d_body[source].astype(BF16), kernel)).astype(F32))
        edge = interleaved(rounded(dot(edge_rows.astype(BF16), kernel)).astype(F32))
        down, upper = shifted(plane, edge, edge, zc)
        up[x] = plane
        ue[x] = jnp.where(fine_half, upper, down)

    loads[4].wait()

    @pl.loop(0, xc)
    def _(x):
        joined = rounded(acc[x] + fine_conv(up, ue, wide_w, 2 * x, 2, size_y, zc))
        result = dot(head_ref[...], joined)
        out_ref[2 * x] = result[:, : yc * zc]
        out_ref[2 * x + 1] = result[:, yc * zc :]

    for copy in coarse_copies + skip_copies + middle_copies + deep_copies:
        copy.wait_send()


def fine_kernel(weight):
    taps = weight.reshape(3, 3, 3, weight.shape[1], weight.shape[2])
    zero = jnp.zeros_like(taps[:, :, 0])
    low = jnp.concatenate([taps[:, :, 1], taps[:, :, 2], zero, taps[:, :, 0]], axis=-1)
    high = jnp.concatenate([taps[:, :, 0], taps[:, :, 1], taps[:, :, 2], zero], axis=-1)
    pair = jnp.concatenate([low, high], axis=2)
    blank = jnp.zeros_like(pair[:, :1])
    wide = jnp.concatenate(
        [jnp.concatenate([pair, blank], axis=1), jnp.concatenate([blank, pair], axis=1)], axis=2
    )
    return wide.reshape(12, wide.shape[2], wide.shape[3])


def local(
    displacement, lift_weight, encode_weight, downward_weight, middle_first, middle_second,
    up_weight, decode_weight, head_weight,
):
    comps, size_x, size_y, size_z = displacement.shape
    c1, c2 = encode_weight.shape[1], middle_first.shape[1]
    xc, yc, zc = size_x // 2, size_y // 2, size_z // 2
    rows_y = -(-(size_y + 2) // 8) * 8

    padded = padded_by(displacement, 2)
    cells = jnp.transpose(padded, (1, 2, 3, 0)).reshape(size_x + 4, size_y + 4, -1)
    rows = jnp.concatenate(
        [
            cells[a : a + size_x + 2, b : b + size_y + 2]
            for a in range(3) for b in range(3)
        ],
        axis=-1,
    )
    depth = rows.shape[-1]
    lanes = -(-depth // 128) * 128
    rows = jnp.pad(rows, ((0, 0), (0, rows_y - size_y - 2), (0, lanes - depth)))
    rows = rows.reshape((size_x + 2) * rows_y, lanes)
    base = jnp.transpose(lift_weight.reshape(9, 3, c1, comps), (2, 0, 1, 3)).reshape(c1, 9, -1)
    base = jnp.pad(base, ((0, 0), (0, 0), (0, depth // 9 - base.shape[-1]))).reshape(c1, depth)
    base = jnp.pad(base, ((0, 0), (0, lanes - depth))).astype(F32)

    encode = fine_kernel(encode_weight)
    skip_w = fine_kernel(decode_weight[:, :, :c1])
    wide_w = fine_kernel(decode_weight[:, :, c1:])
    downward = jnp.transpose(downward_weight.reshape(2, 4, c2, c1), (0, 2, 1, 3)).reshape(
        2, c2, 4 * c1
    )
    up_w = up_weight.reshape(4, 2 * c1, c2)
    head = jnp.einsum("pq,ki->pkqi", jnp.eye(4, dtype=BF16), head_weight).reshape(
        4 * comps, 4 * c1
    )
    head = jnp.pad(head, ((0, 16 - 4 * comps), (0, 0)))

    def coarse_set():
        return [
            pltpu.VMEM((xc + 2, (yc + 2) * zc, 128), F32),
            pltpu.VMEM((xc + 2, yc + 2, 1, 128), F32),
            pltpu.VMEM((xc + 2, yc + 2, 1, 128), F32),
            pltpu.VMEM((xc, yc, 1, 128), F32),
            pltpu.VMEM((xc, yc, 1, 128), F32),
        ]

    fine = pltpu.VMEM((size_x + 2, (size_y + 2) * zc, 128), F32)
    first = pltpu.VMEM((size_x + 2, rows_y * zc, 128), F32)
    vmem, anywhere = pl.BlockSpec(memory_space=pltpu.VMEM), pl.BlockSpec(memory_space=pl.ANY)
    result = pl.pallas_call(
        functools.partial(unet, (size_x, size_y, size_z, rows_y)),
        out_shape=jax.ShapeDtypeStruct((size_x, 16, yc * zc), F32),
        in_specs=[
            vmem, vmem, anywhere, vmem, anywhere, anywhere, vmem, anywhere, anywhere, vmem
        ],
        out_specs=vmem,
        scratch_shapes=[
            pltpu.VMEM((zc + 1, (size_x + 2) * rows_y, 128), F32),
            first, first, fine, fine, fine, fine,
            pltpu.VMEM((xc, 2 * yc * zc, 4 * c1), F32),
            pltpu.VMEM((size_x + 2, size_y + 2, 1, 128), F32),
            pltpu.VMEM((size_x + 2, size_y + 2, 1, 128), F32),
            pltpu.VMEM((size_x, size_y, 1, 128), F32),
            pltpu.VMEM((size_x, size_y, 1, 128), F32),
            coarse_set(), coarse_set(), coarse_set(),
            pltpu.VMEM((xc + 2, (yc + 2) * zc, 128), F32),
            pltpu.VMEM((xc + 2, (yc + 2) * zc, 128), F32),
            pltpu.VMEM(encode.shape, BF16),
            pltpu.VMEM(middle_first.shape, BF16),
            pltpu.VMEM(middle_second.shape, BF16),
            pltpu.VMEM(skip_w.shape, BF16),
            pltpu.VMEM(wide_w.shape, BF16),
            pltpu.SemaphoreType.DMA((5,)),
            pltpu.SemaphoreType.DMA((4, len(DIRS))),
            pltpu.SemaphoreType.DMA((4, len(DIRS))),
        ],
        compiler_params=pltpu.CompilerParams(
            collective_id=0, has_side_effects=True, vmem_limit_bytes=40 * 2**20
        ),
    )(rows, base, encode, downward, middle_first, middle_second, up_w, skip_w, wide_w, head)
    head_out = result[:, : 4 * comps].reshape(size_x, 2, 2, comps, yc, zc)
    head_out = jnp.transpose(head_out, (3, 0, 4, 1, 5, 2)).reshape(displacement.shape)
    return displacement.astype(F32) + head_out


def solution(mesh):
    placed = (P(None, "gx", "gy", "gz"), P(), P(), P(), P(), P(), P(), P(), P())
    return jax.shard_map(
        local, mesh=mesh, in_specs=placed, out_specs=P(None, "gx", "gy", "gz"), check_vma=False
    )
```

```python
import functools

import jax
import jax.numpy as jnp
from jax import lax
from jax.experimental import pallas as pl
from jax.experimental.pallas import tpu as pltpu
from jax.sharding import PartitionSpec as P

AXES = ("gx", "gy", "gz")
MESH = pl.DeviceIdType.MESH
NT = (((1,), (1,)), ((), ()))
DIRS = [
    (dx, dy, dz) for dx in (-1, 0, 1) for dy in (-1, 0, 1) for dz in (-1, 0, 1)
    if (dx, dy, dz) != (0, 0, 0)
]
F32, BF16 = jnp.float32, jnp.bfloat16
RIM = 16


def leaky(value):
    return jnp.maximum(value, 0.1 * value)


def rounded(value):
    return leaky(value).astype(BF16)


def dot(rows, weight):
    return lax.dot_general(rows, weight, NT, preferred_element_type=F32)


def neighbour(direction):
    return tuple(
        lax.rem(lax.axis_index(axis) + lax.axis_size(axis) + step, lax.axis_size(axis))
        for axis, step in zip(AXES, direction)
    )


def exchange(body, below, above, first, last, sends, recvs, zc):
    size_x, size_y = body.shape[0] - 2, body.shape[1] // zc - 2
    copies = []
    for number, (dx, dy, dz) in enumerate(DIRS):
        def span(step, size, offset):
            if step == 0:
                return (offset, size, 1)
            return (offset + size - 1, 1, 0) if step > 0 else (offset, 1, size + 1)

        if dz == 0:
            sx, nx, tx = span(dx, size_x, 1)
            sy, ny, ty = span(dy, size_y, 1)
            src = body.at[pl.ds(sx, nx), pl.ds(sy * zc, ny * zc)]
            dst = body.at[pl.ds(tx, nx), pl.ds(ty * zc, ny * zc)]
        else:
            sx, nx, tx = span(dx, size_x, 0)
            sy, ny, ty = span(dy, size_y, 0)
            src = (last if dz > 0 else first).at[pl.ds(sx, nx), pl.ds(sy, ny)]
            dst = (below if dz > 0 else above).at[pl.ds(tx, nx), pl.ds(ty, ny)]
        copies.append(
            pltpu.make_async_remote_copy(
                src_ref=src, dst_ref=dst, send_sem=sends.at[number], recv_sem=recvs.at[number],
                device_id=neighbour((dx, dy, dz)), device_id_type=MESH,
            )
        )
    for copy in copies:
        copy.start()
    return copies


def send_cells(cells, block, sends, recvs):
    size_x, size_y = cells.shape[:2]
    copies = []
    for number, (dx, dy, dz) in enumerate(DIRS):
        sx, nx, tx = {0: (0, size_x, 2), 1: (size_x - 2, 2, 0), -1: (0, 2, size_x + 2)}[dx]
        sy, ny, ty = {
            0: (0, size_y, RIM), 1: (size_y - RIM, RIM, 0), -1: (0, RIM, size_y + RIM)
        }[dy]
        copies.append(
            pltpu.make_async_remote_copy(
                src_ref=cells.at[pl.ds(sx, nx), pl.ds(sy, ny)],
                dst_ref=block.at[1 - dz, pl.ds(tx, nx), pl.ds(ty, ny)],
                send_sem=sends.at[number], recv_sem=recvs.at[number],
                device_id=neighbour((dx, dy, dz)), device_id_type=MESH,
            )
        )
    for copy in copies:
        copy.start()
    return copies


def build_fine(raw, wide, lo, hi):
    out = raw.shape[1]
    blank = jnp.zeros((2 * out, wide.shape[2]), BF16)
    zero = jnp.zeros((out, hi - lo), BF16)
    for a in range(3):
        wide[4 * a, 2 * out :, :] = blank
        wide[4 * a + 3, : 2 * out, :] = blank
        for b in range(3):
            taps = [raw[9 * a + 3 * b + c][:, lo:hi] for c in range(3)]
            low = jnp.concatenate([taps[1], taps[2], zero, taps[0]], axis=1)
            high = jnp.concatenate([taps[0], taps[1], taps[2], zero], axis=1)
            pair = jnp.concatenate([low, high], axis=0)
            wide[4 * a + b, : 2 * out, :] = pair
            wide[4 * a + b + 1, 2 * out :, :] = pair


def masks(rows, zc):
    row = lax.rem(lax.broadcasted_iota(jnp.int32, (rows, 128), 0), zc)
    return row == 0, row == zc - 1


def half_mask(rows):
    return lax.broadcasted_iota(jnp.int32, (rows, 128), 1) < 64


def spread(edge, zc):
    return jnp.broadcast_to(edge, (edge.shape[0], zc, 128)).reshape(edge.shape[0] * zc, 128)


def shifted(plane, below, above, zc):
    rows = plane.shape[0]
    start, end = masks(rows, zc)
    down = jnp.where(start, below, pltpu.roll(plane, 1, 0))
    up = jnp.where(end, above, pltpu.roll(plane, rows - 1, 0))
    return down, up


def fine_conv(plane, twin, weight, x0, group, size_y, zc):
    summed = None
    pairs = size_y // 2
    for a in range(3):
        parts = []
        for source in (plane, twin):
            halves = [[], []]
            for g in range(group):
                value = source[x0 + g + a, pl.ds(0, (size_y + 2) * zc), :]
                value = value.reshape(pairs + 1, 2, zc, 128)
                halves[0].append(value[:, 0])
                halves[1].append(value[:, 1])
            parts.append(halves)
        for b in range(4):
            cut = [
                jnp.concatenate(
                    [
                        v[b // 2 : b // 2 + pairs].reshape(pairs * zc, 128)
                        for v in halves[b % 2]
                    ],
                    axis=0,
                ).astype(BF16)
                for halves in parts
            ]
            term = dot(jnp.concatenate(cut, axis=1), weight[4 * a + b])
            summed = term if summed is None else summed + term
    return summed


def coarse_conv(body, low, high, weight, zc):
    size_x, rows = body.shape[0] - 2, body.shape[1] - 2 * zc
    summed = None
    for a in range(3):
        for b in range(3):
            lhs = jnp.concatenate(
                [
                    jnp.concatenate(
                        [ref[x + a, pl.ds(b * zc, rows), :] for x in range(size_x)], axis=0
                    ).astype(BF16)
                    for ref in (low, body, high)
                ],
                axis=1,
            )
            tap = 9 * a + 3 * b
            kernel = jnp.concatenate([weight[tap], weight[tap + 1], weight[tap + 2]], axis=1)
            term = dot(lhs, kernel)
            summed = term if summed is None else summed + term
    return summed


def unet(
    sizes,
    cells_ref, lift_ref, encode_hbm, downward_hbm, first_hbm, second_hbm, up_hbm,
    decode_hbm, head_ref,
    out_ref,
    block, joint, lhs32, lhs16, chunks, fp, fe, sp, se, up, ue, acc,
    s_below, s_above, s_first, s_last,
    coarse_bufs, middle_bufs, deep_bufs, low, high,
    encode_raw, downward_raw, first_w, second_w, up_ref, decode_raw,
    encode_w, skip_w, wide_w,
    load_sems, send_sems, recv_sems,
):
    comps, size_x, size_y, size_z, rows_y = sizes
    zc, yc, xc = size_z // 2, size_y // 2, size_x // 2
    loads = [
        pltpu.make_async_copy(src, dst, load_sems.at[i])
        for i, (src, dst) in enumerate(
            (
                (encode_hbm, encode_raw), (downward_hbm, downward_raw), (first_hbm, first_w),
                (decode_hbm, decode_raw), (second_hbm, second_w), (up_hbm, up_ref),
            )
        )
    ]
    for load in loads:
        load.start()
    barrier = pltpu.get_barrier_semaphore()
    for direction in DIRS:
        pl.semaphore_signal(barrier, inc=1, device_id=neighbour(direction), device_id_type=MESH)
    pl.semaphore_wait(barrier, len(DIRS))
    cell_copies = send_cells(cells_ref, block, send_sems.at[4], recv_sems.at[4])
    block[1, pl.ds(2, size_x), pl.ds(RIM, size_y), :] = cells_ref[...]

    groups = []
    for g in range(5):
        total = None
        for tap in range(2 * g, min(2 * g + 2, 9)):
            for c in range(3):
                piece = lift_ref[3 * tap + c].astype(F32)
                shift = 64 * (tap % 2) + comps * c
                piece = pltpu.roll(piece, shift, 1) if shift else piece
                total = piece if total is None else total + piece
        groups.append(total)
    loads[0].wait()
    build_fine(encode_raw, encode_w, 0, encode_raw.shape[2])
    loads[1].wait()
    downward = [
        jnp.concatenate([downward_raw[4 * a + t] for t in range(4)], axis=1) for a in range(2)
    ]
    for copy in cell_copies:
        copy.wait_recv()

    width = comps * size_z
    edge = 2 * comps
    all_rows = size_y + 2 * RIM
    lane = lax.broadcasted_iota(jnp.int32, (all_rows, 128), 1)
    for x in range(size_x + 4):
        own = pltpu.roll(block[1, x].astype(F32), edge, 1)
        before = pltpu.roll(block[0, x].astype(F32), 128 - (width - edge), 1)
        after = pltpu.roll(block[2, x].astype(F32), width + edge, 1)
        joint[x] = jnp.where(
            lane < edge,
            before,
            jnp.where(lane < edge + width, own, jnp.where(lane < width + 2 * edge, after, 0.0)),
        )
    half = half_mask(rows_y)
    for x in range(size_x + 2):
        for g in range(5):
            parts = [
                joint[x + tap // 3, pl.ds(RIM - 2 + tap % 3, rows_y), :]
                for tap in range(2 * g, min(2 * g + 2, 9))
            ]
            other = pltpu.roll(parts[1], 64, 1) if len(parts) > 1 else jnp.zeros_like(parts[0])
            lhs32[pl.ds(x * rows_y, rows_y), 128 * g : 128 * g + 128] = jnp.where(
                half, parts[0], other
            )
    lhs16[...] = lhs32[...].astype(BF16)

    for p in range(zc + 1):
        z_lo, z_hi = (2 * p, 2 * p + 1) if p < zc else (size_z, -1)
        kernel = jnp.concatenate(
            [
                jnp.concatenate(
                    [pltpu.roll(v, comps * (z + 1), 1) if z + 1 else v for v in groups], axis=1
                )
                for z in (z_lo, z_hi)
            ],
            axis=0,
        ).astype(BF16)
        chunks[p] = rounded(dot(lhs16[...], kernel)).astype(F32)
    for x in range(size_x + 2):
        span = pl.ds(x * rows_y, rows_y)
        for p in range(zc):
            fp[x, pl.ds(p, rows_y, stride=zc), :] = chunks[p, span, :]
            fe[x, pl.ds(p, rows_y, stride=zc), :] = jnp.where(
                half, chunks[p + 1, span, :], chunks[zc if p == 0 else p - 1, span, :]
            )

    c_body, c_below, c_above, c_first, c_last = coarse_bufs
    m_body, m_below, m_above, m_first, m_last = middle_bufs
    d_body, d_below, d_above, d_first, d_last = deep_bufs

    @pl.loop(0, xc)
    def _(x):
        skip = rounded(fine_conv(fp, fe, encode_w, 2 * x, 2, size_y, zc))
        half_rows = yc * zc
        coarse = None
        for g in range(2):
            part = skip[g * half_rows : (g + 1) * half_rows]
            term = dot(part, downward[g])
            coarse = term if coarse is None else coarse + term
            wide = part.astype(F32)
            plane = jnp.stack(
                [wide[:, :128].reshape(yc, zc, 128), wide[:, 128:].reshape(yc, zc, 128)], axis=1
            ).reshape(size_y, zc, 128)
            sp[2 * x + g + 1, pl.ds(zc, size_y * zc), :] = plane.reshape(size_y * zc, 128)
            s_first[2 * x + g] = plane[:, 0:1, :]
            s_last[2 * x + g] = plane[:, zc - 1 : zc, :]
        coarse = rounded(coarse).astype(F32)
        c_body[x + 1, pl.ds(zc, half_rows), :] = coarse
        c_first[x] = coarse.reshape(yc, zc, 128)[:, 0:1, :]
        c_last[x] = coarse.reshape(yc, zc, 128)[:, zc - 1 : zc, :]

    coarse_copies = exchange(*coarse_bufs, send_sems.at[0], recv_sems.at[0], zc)
    skip_copies = exchange(
        sp, s_below, s_above, s_first, s_last, send_sems.at[1], recv_sems.at[1], zc
    )

    def coarse_layer(bufs, weight, result):
        body, below, above = bufs[:3]
        for x in range(xc + 2):
            down, upper = shifted(body[x], spread(below[x], zc), spread(above[x], zc), zc)
            low[x] = down
            high[x] = upper
        value = rounded(coarse_conv(body, low, high, weight, zc)).astype(F32)
        target, _, _, first, last = result
        for x in range(xc):
            part = value[x * yc * zc : (x + 1) * yc * zc]
            target[x + 1, pl.ds(zc, yc * zc), :] = part
            first[x] = part.reshape(yc, zc, 128)[:, 0:1, :]
            last[x] = part.reshape(yc, zc, 128)[:, zc - 1 : zc, :]

    loads[2].wait()
    loads[3].wait()
    channels = decode_raw.shape[2] // 2
    build_fine(decode_raw, skip_w, 0, channels)
    build_fine(decode_raw, wide_w, channels, 2 * channels)
    for copy in coarse_copies:
        copy.wait_recv()
    coarse_layer(coarse_bufs, first_w, middle_bufs)
    middle_copies = exchange(*middle_bufs, send_sems.at[2], recv_sems.at[2], zc)

    for copy in middle_copies:
        copy.wait_recv()
    loads[4].wait()
    coarse_layer(middle_bufs, second_w, deep_bufs)
    deep_copies = exchange(*deep_bufs, send_sems.at[3], recv_sems.at[3], zc)

    for copy in skip_copies:
        copy.wait_recv()
    fine_half = half_mask((size_y + 2) * zc)

    @pl.loop(0, size_x + 2)
    def _(x):
        down, upper = shifted(sp[x], spread(s_below[x], zc), spread(s_above[x], zc), zc)
        se[x] = jnp.where(fine_half, upper, down)

    loads[5].wait()

    @pl.loop(0, xc)
    def _(x):
        acc[x] = fine_conv(sp, se, skip_w, 2 * x, 2, size_y, zc)

    for copy in deep_copies:
        copy.wait_recv()
    coarse_rows = (yc + 2) * zc
    _, coarse_end = masks(coarse_rows, zc)

    def interleaved(value):
        even = value[:, 128:].reshape(yc + 2, zc, 128)[: yc + 1]
        odd = value[:, :128].reshape(yc + 2, zc, 128)[1:]
        return jnp.stack([even, odd], axis=1).reshape((size_y + 2) * zc, 128)

    for x in range(size_x + 2):
        source, a = (x + 1) // 2, (x + 1) % 2
        kernel = jnp.concatenate([up_ref[2 * a], up_ref[2 * a + 1]], axis=0)
        edge_rows = jnp.where(
            coarse_end, spread(d_above[source], zc), spread(d_below[source], zc)
        )
        plane = interleaved(rounded(dot(d_body[source].astype(BF16), kernel)).astype(F32))
        edge = interleaved(rounded(dot(edge_rows.astype(BF16), kernel)).astype(F32))
        down, upper = shifted(plane, edge, edge, zc)
        up[x] = plane
        ue[x] = jnp.where(fine_half, upper, down)

    @pl.loop(0, xc)
    def _(x):
        joined = rounded(acc[x] + fine_conv(up, ue, wide_w, 2 * x, 2, size_y, zc))
        result = dot(head_ref[...], joined)
        out_ref[2 * x] = result[:, : yc * zc]
        out_ref[2 * x + 1] = result[:, yc * zc :]

    for copy in cell_copies + coarse_copies + skip_copies + middle_copies + deep_copies:
        copy.wait_send()


def local(
    displacement, lift_weight, encode_weight, downward_weight, middle_first, middle_second,
    up_weight, decode_weight, head_weight,
):
    comps, size_x, size_y, size_z = displacement.shape
    c1, c2 = encode_weight.shape[1], middle_first.shape[1]
    xc, yc, zc = size_x // 2, size_y // 2, size_z // 2
    rows_y = -(-(size_y + 2) // 8) * 8

    cells = jnp.transpose(displacement, (1, 2, 3, 0)).reshape(size_x, size_y, -1)
    cells = jnp.pad(cells, ((0, 0), (0, 0), (0, 128 - cells.shape[-1])))
    lift = jnp.pad(lift_weight, ((0, 0), (0, 0), (0, 128 - comps)))
    up_w = up_weight.reshape(4, 2 * c1, c2)
    head = jnp.einsum("pq,ki->pkqi", jnp.eye(4, dtype=BF16), head_weight).reshape(
        4 * comps, 4 * c1
    )
    head = jnp.pad(head, ((0, 16 - 4 * comps), (0, 0)))

    def coarse_set():
        return [
            pltpu.VMEM((xc + 2, (yc + 2) * zc, 128), F32),
            pltpu.VMEM((xc + 2, yc + 2, 1, 128), F32),
            pltpu.VMEM((xc + 2, yc + 2, 1, 128), F32),
            pltpu.VMEM((xc, yc, 1, 128), F32),
            pltpu.VMEM((xc, yc, 1, 128), F32),
        ]

    fine = pltpu.VMEM((size_x + 2, (size_y + 2) * zc, 128), F32)
    first = pltpu.VMEM((size_x + 2, rows_y * zc, 128), F32)
    vmem, anywhere = pl.BlockSpec(memory_space=pltpu.VMEM), pl.BlockSpec(memory_space=pltpu.HBM)
    result = pl.pallas_call(
        functools.partial(unet, (comps, size_x, size_y, size_z, rows_y)),
        out_shape=jax.ShapeDtypeStruct((size_x, 16, yc * zc), F32),
        in_specs=[vmem, vmem] + [anywhere] * 6 + [vmem],
        out_specs=vmem,
        scratch_shapes=[
            pltpu.VMEM((3, size_x + 4, size_y + 2 * RIM, 128), BF16),
            pltpu.VMEM((size_x + 4, size_y + 2 * RIM, 128), F32),
            pltpu.VMEM(((size_x + 2) * rows_y, 640), F32),
            pltpu.VMEM(((size_x + 2) * rows_y, 640), BF16),
            pltpu.VMEM((zc + 1, (size_x + 2) * rows_y, 128), F32),
            first, first, fine, fine, fine, fine,
            pltpu.VMEM((xc, 2 * yc * zc, 4 * c1), F32),
            pltpu.VMEM((size_x + 2, size_y + 2, 1, 128), F32),
            pltpu.VMEM((size_x + 2, size_y + 2, 1, 128), F32),
            pltpu.VMEM((size_x, size_y, 1, 128), F32),
            pltpu.VMEM((size_x, size_y, 1, 128), F32),
            coarse_set(), coarse_set(), coarse_set(),
            pltpu.VMEM((xc + 2, (yc + 2) * zc, 128), F32),
            pltpu.VMEM((xc + 2, (yc + 2) * zc, 128), F32),
            pltpu.VMEM(encode_weight.shape, BF16),
            pltpu.VMEM(downward_weight.shape, BF16),
            pltpu.VMEM(middle_first.shape, BF16),
            pltpu.VMEM(middle_second.shape, BF16),
            pltpu.VMEM(up_w.shape, BF16),
            pltpu.VMEM(decode_weight.shape, BF16),
            pltpu.VMEM((12, 4 * c1, 4 * c1), BF16),
            pltpu.VMEM((12, 4 * c1, 4 * c1), BF16),
            pltpu.VMEM((12, 4 * c1, 4 * c1), BF16),
            pltpu.SemaphoreType.DMA((6,)),
            pltpu.SemaphoreType.DMA((5, len(DIRS))),
            pltpu.SemaphoreType.DMA((5, len(DIRS))),
        ],
        compiler_params=pltpu.CompilerParams(
            collective_id=0, has_side_effects=True, vmem_limit_bytes=40 * 2**20
        ),
    )(
        cells, lift, encode_weight, downward_weight, middle_first, middle_second, up_w,
        decode_weight, head,
    )
    head_out = result[:, : 4 * comps].reshape(size_x, 2, 2, comps, yc, zc)
    head_out = jnp.transpose(head_out, (3, 0, 4, 1, 5, 2)).reshape(displacement.shape)
    return displacement.astype(F32) + head_out


def solution(mesh):
    placed = (P(None, "gx", "gy", "gz"), P(), P(), P(), P(), P(), P(), P(), P())
    return jax.shard_map(
        local, mesh=mesh, in_specs=placed, out_specs=P(None, "gx", "gy", "gz"), check_vma=False
    )
```

```python
import functools

import jax
import jax.numpy as jnp
from jax import lax
from jax.experimental import pallas as pl
from jax.experimental.pallas import tpu as pltpu
from jax.sharding import PartitionSpec as P

AXES = ("gx", "gy", "gz")
MESH = pl.DeviceIdType.MESH
NT = (((1,), (1,)), ((), ()))
DIRS = [
    (dx, dy, dz) for dx in (-1, 0, 1) for dy in (-1, 0, 1) for dz in (-1, 0, 1)
    if (dx, dy, dz) != (0, 0, 0)
]
F32, BF16 = jnp.float32, jnp.bfloat16
RIM = 8


def leaky(value):
    return jnp.maximum(value, 0.1 * value)


def rounded(value):
    return leaky(value).astype(BF16)


def dot(rows, weight):
    return lax.dot_general(rows, weight, NT, preferred_element_type=F32)


def neighbour(direction):
    return tuple(
        lax.rem(lax.axis_index(axis) + lax.axis_size(axis) + step, lax.axis_size(axis))
        for axis, step in zip(AXES, direction)
    )


def exchange(body, below, above, first, last, sends, recvs, zc):
    size_x, size_y = body.shape[0] - 2, body.shape[1] - 2
    copies = []
    for number, (dx, dy, dz) in enumerate(DIRS):
        def span(step, size, offset):
            if step == 0:
                return (offset, size, 1)
            return (offset + size - 1, 1, 0) if step > 0 else (offset, 1, size + 1)

        if dz == 0:
            sx, nx, tx = span(dx, size_x, 1)
            sy, ny, ty = span(dy, size_y, 1)
            src = body.at[pl.ds(sx, nx), pl.ds(sy, ny)]
            dst = body.at[pl.ds(tx, nx), pl.ds(ty, ny)]
        else:
            sx, nx, tx = span(dx, size_x, 0)
            sy, ny, ty = span(dy, size_y, 0)
            src = (last if dz > 0 else first).at[pl.ds(sx, nx), pl.ds(sy, ny)]
            dst = (below if dz > 0 else above).at[pl.ds(tx, nx), pl.ds(ty, ny)]
        copies.append(
            pltpu.make_async_remote_copy(
                src_ref=src, dst_ref=dst, send_sem=sends.at[number], recv_sem=recvs.at[number],
                device_id=neighbour((dx, dy, dz)), device_id_type=MESH,
            )
        )
    for copy in copies:
        copy.start()
    return copies


def send_cells(block, before, after, first, last, sends, recvs):
    size_x, size_y = block.shape[0] - 4, block.shape[1] - 2
    copies = []
    for number, (dx, dy, dz) in enumerate(DIRS):
        sx, nx, tx = {0: (2, size_x, 2), 1: (size_x, 2, 0), -1: (2, 2, size_x + 2)}[dx]
        sy, ny, ty = {0: (0, size_y, 1), 1: (size_y - 1, 1, 0), -1: (0, 1, size_y + 1)}[dy]
        if dz == 0:
            src = block.at[pl.ds(sx, nx), pl.ds(sy + 1, ny)]
            dst = block.at[pl.ds(tx, nx), pl.ds(ty, ny)]
        else:
            src = (last if dz > 0 else first).at[pl.ds(sy, ny)]
            dst = (before if dz > 0 else after).at[1 - dx, pl.ds(ty, ny)]
        copies.append(
            pltpu.make_async_remote_copy(
                src_ref=src, dst_ref=dst, send_sem=sends.at[number], recv_sem=recvs.at[number],
                device_id=neighbour((dx, dy, dz)), device_id_type=MESH,
            )
        )
    for copy in copies:
        copy.start()
    return copies


def build_fine(raw, wide, lo, hi):
    out = raw.shape[1]
    blank = jnp.zeros((2 * out, wide.shape[2]), BF16)
    zero = jnp.zeros((out, hi - lo), BF16)
    for a in range(3):
        wide[4 * a, 2 * out :, :] = blank
        wide[4 * a + 3, : 2 * out, :] = blank
        for b in range(3):
            taps = [raw[9 * a + 3 * b + c][:, lo:hi] for c in range(3)]
            low = jnp.concatenate([taps[1], taps[2], zero, taps[0]], axis=1)
            high = jnp.concatenate([taps[0], taps[1], taps[2], zero], axis=1)
            pair = jnp.concatenate([low, high], axis=0)
            wide[4 * a + b, : 2 * out, :] = pair
            wide[4 * a + b + 1, 2 * out :, :] = pair


def masks(rows, zc):
    row = lax.rem(lax.broadcasted_iota(jnp.int32, (rows, 128), 0), zc)
    return row == 0, row == zc - 1


def half_mask(rows):
    return lax.broadcasted_iota(jnp.int32, (rows, 128), 1) < 64


def flat(plane):
    return plane.astype(F32).reshape(plane.shape[0] * plane.shape[1], 128)


def spread(edge, zc):
    return jnp.broadcast_to(edge, (edge.shape[0], zc, 128)).reshape(edge.shape[0] * zc, 128)


def shifted(plane, below, above, zc):
    rows = plane.shape[0]
    start, end = masks(rows, zc)
    down = jnp.where(start, below, pltpu.roll(plane, 1, 0))
    up = jnp.where(end, above, pltpu.roll(plane, rows - 1, 0))
    return down, up


def fine_conv(plane, twin, weight, x0, group, size_y, zc):
    summed = None
    pairs = size_y // 2
    for a in range(3):
        parts = []
        for source in (plane, twin):
            halves = [[], []]
            for g in range(group):
                value = source[x0 + g + a, pl.ds(0, (size_y + 2) * zc), :]
                value = value.reshape(pairs + 1, 2, zc, 128)
                halves[0].append(value[:, 0])
                halves[1].append(value[:, 1])
            parts.append(halves)
        for b in range(4):
            cut = [
                jnp.concatenate(
                    [
                        v[b // 2 : b // 2 + pairs].reshape(pairs * zc, 128)
                        for v in halves[b % 2]
                    ],
                    axis=0,
                ).astype(BF16)
                for halves in parts
            ]
            term = dot(jnp.concatenate(cut, axis=1), weight[4 * a + b])
            summed = term if summed is None else summed + term
    return summed


def coarse_conv(body, low, high, weight, zc):
    size_x, rows = body.shape[0] - 2, body.shape[1] - 2 * zc
    summed = None
    for a in range(3):
        for b in range(3):
            lhs = jnp.concatenate(
                [
                    jnp.concatenate(
                        [ref[x + a, pl.ds(b * zc, rows), :] for x in range(size_x)], axis=0
                    ).astype(BF16)
                    for ref in (low, body, high)
                ],
                axis=1,
            )
            tap = 9 * a + 3 * b
            kernel = jnp.concatenate([weight[tap], weight[tap + 1], weight[tap + 2]], axis=1)
            term = dot(lhs, kernel)
            summed = term if summed is None else summed + term
    return summed


def unet(
    sizes,
    cells_ref, lift_ref, encode_hbm, downward_hbm, first_hbm, second_hbm, up_hbm,
    decode_hbm, head_ref,
    out_ref,
    block, before, after, cell_first, cell_last, joint, lhs32, lhs16, chunks, fp, fe, sp, sf, se, up, ue, acc,
    s_below, s_above, s_first, s_last,
    coarse_bufs, middle_bufs, deep_bufs, low, middle, high,
    encode_raw, downward_raw, first_w, second_w, up_ref, decode_raw,
    encode_w, skip_w, wide_w,
    load_sems, send_sems, recv_sems,
):
    comps, size_x, size_y, size_z, rows_y = sizes
    zc, yc, xc = size_z // 2, size_y // 2, size_x // 2
    loads = [
        pltpu.make_async_copy(src, dst, load_sems.at[i])
        for i, (src, dst) in enumerate(
            (
                (encode_hbm, encode_raw), (downward_hbm, downward_raw), (first_hbm, first_w),
                (decode_hbm, decode_raw), (second_hbm, second_w), (up_hbm, up_ref),
            )
        )
    ]
    for load in loads:
        load.start()
    barrier = pltpu.get_barrier_semaphore()
    for direction in DIRS:
        pl.semaphore_signal(barrier, inc=1, device_id=neighbour(direction), device_id_type=MESH)
    width, edge = comps * size_z, 2 * comps
    own_rows = lax.broadcasted_iota(jnp.int32, (size_y, 128), 1)
    rims = [None, None]
    for x in range(size_x):
        value = cells_ref[x].astype(F32)
        block[x + 2, pl.ds(1, size_y // RIM)] = value.reshape(size_y // RIM, RIM, 128).astype(
            BF16
        )
        for side, start in enumerate((0, width - edge)):
            kept = jnp.where((own_rows >= start) & (own_rows < start + edge), value, 0.0)
            shift = (edge * x - start) % 128
            kept = pltpu.roll(kept, shift, 1) if shift else kept
            rims[side] = kept if rims[side] is None else rims[side] + kept
    cell_first[...] = rims[0].reshape(size_y // RIM, RIM, 128).astype(BF16)
    cell_last[...] = rims[1].reshape(size_y // RIM, RIM, 128).astype(BF16)
    pl.semaphore_wait(barrier, len(DIRS))
    cell_copies = send_cells(
        block, before, after, cell_first, cell_last, send_sems.at[4], recv_sems.at[4]
    )

    groups = []
    for g in range(5):
        total = None
        for tap in range(2 * g, min(2 * g + 2, 9)):
            for c in range(3):
                piece = lift_ref[3 * tap + c].astype(F32)
                shift = 64 * (tap % 2) + comps * c
                piece = pltpu.roll(piece, shift, 1) if shift else piece
                total = piece if total is None else total + piece
        groups.append(total)
    loads[0].wait()
    build_fine(encode_raw, encode_w, 0, encode_raw.shape[2])
    loads[1].wait()
    downward = [
        jnp.concatenate([downward_raw[4 * a + t] for t in range(4)], axis=1) for a in range(2)
    ]
    for copy in cell_copies:
        copy.wait_recv()

    all_rows = size_y + 2 * RIM
    lane = lax.broadcasted_iota(jnp.int32, (all_rows, 128), 1)

    def turned(value, shift):
        return pltpu.roll(value, shift % 128, 1) if shift % 128 else value

    for x in range(size_x + 4):
        near, place = (
            (0, size_x - 2 + x) if x < 2 else (1, x - 2) if x < size_x + 2
            else (2, x - size_x - 2)
        )
        own = turned(flat(block[x]), edge)
        before_x = turned(flat(before[near]), -edge * place)
        after_x = turned(flat(after[near]), width + edge - edge * place)
        joint[x] = jnp.where(
            lane < edge,
            before_x,
            jnp.where(lane < edge + width, own, jnp.where(lane < width + 2 * edge, after_x, 0.0)),
        )
    half = half_mask(rows_y)
    for x in range(size_x + 2):
        for g in range(5):
            parts = [
                joint[x + tap // 3, pl.ds(RIM - 2 + tap % 3, rows_y), :]
                for tap in range(2 * g, min(2 * g + 2, 9))
            ]
            other = pltpu.roll(parts[1], 64, 1) if len(parts) > 1 else jnp.zeros_like(parts[0])
            lhs32[pl.ds(x * rows_y, rows_y), 128 * g : 128 * g + 128] = jnp.where(
                half, parts[0], other
            )
    lhs16[...] = lhs32[...].astype(BF16)

    for p in range(zc + 1):
        z_lo, z_hi = (2 * p, 2 * p + 1) if p < zc else (size_z, -1)
        kernel = jnp.concatenate(
            [
                jnp.concatenate(
                    [pltpu.roll(v, comps * (z + 1), 1) if z + 1 else v for v in groups], axis=1
                )
                for z in (z_lo, z_hi)
            ],
            axis=0,
        ).astype(BF16)
        chunks[p] = rounded(dot(lhs16[...], kernel)).astype(F32)
    for x in range(size_x + 2):
        span = pl.ds(x * rows_y, rows_y)
        for p in range(zc):
            fp[x, pl.ds(p, rows_y, stride=zc), :] = chunks[p, span, :]
            fe[x, pl.ds(p, rows_y, stride=zc), :] = jnp.where(
                half, chunks[p + 1, span, :], chunks[zc if p == 0 else p - 1, span, :]
            )

    c_body, c_below, c_above, c_first, c_last = coarse_bufs
    m_body, m_below, m_above, m_first, m_last = middle_bufs
    d_body, d_below, d_above, d_first, d_last = deep_bufs

    @pl.loop(0, xc)
    def _(x):
        skip = rounded(fine_conv(fp, fe, encode_w, 2 * x, 2, size_y, zc))
        half_rows = yc * zc
        coarse = None
        for g in range(2):
            part = skip[g * half_rows : (g + 1) * half_rows]
            term = dot(part, downward[g])
            coarse = term if coarse is None else coarse + term
            wide = part.astype(F32)
            plane = jnp.stack(
                [wide[:, :128].reshape(yc, zc, 128), wide[:, 128:].reshape(yc, zc, 128)], axis=1
            ).reshape(size_y, zc, 128)
            sp[2 * x + g + 1, pl.ds(1, size_y)] = plane.astype(BF16)
            s_first[2 * x + g] = plane[:, 0:1, :]
            s_last[2 * x + g] = plane[:, zc - 1 : zc, :]
        coarse = rounded(coarse).astype(F32)
        c_body[x + 1, pl.ds(1, yc)] = coarse.reshape(yc, zc, 128).astype(BF16)
        c_first[x] = coarse.reshape(yc, zc, 128)[:, 0:1, :]
        c_last[x] = coarse.reshape(yc, zc, 128)[:, zc - 1 : zc, :]

    coarse_copies = exchange(*coarse_bufs, send_sems.at[0], recv_sems.at[0], zc)
    skip_copies = exchange(
        sp, s_below, s_above, s_first, s_last, send_sems.at[1], recv_sems.at[1], zc
    )

    def coarse_layer(bufs, weight, result):
        body, below, above = bufs[:3]
        for x in range(xc + 2):
            middle[x] = flat(body[x])
            down, upper = shifted(middle[x], spread(below[x], zc), spread(above[x], zc), zc)
            low[x] = down
            high[x] = upper
        value = rounded(coarse_conv(middle, low, high, weight, zc)).astype(F32)
        target, _, _, first, last = result
        for x in range(xc):
            part = value[x * yc * zc : (x + 1) * yc * zc]
            target[x + 1, pl.ds(1, yc)] = part.reshape(yc, zc, 128).astype(BF16)
            first[x] = part.reshape(yc, zc, 128)[:, 0:1, :]
            last[x] = part.reshape(yc, zc, 128)[:, zc - 1 : zc, :]

    loads[2].wait()
    loads[3].wait()
    channels = decode_raw.shape[2] // 2
    build_fine(decode_raw, skip_w, 0, channels)
    build_fine(decode_raw, wide_w, channels, 2 * channels)
    for copy in coarse_copies:
        copy.wait_recv()
    coarse_layer(coarse_bufs, first_w, middle_bufs)
    middle_copies = exchange(*middle_bufs, send_sems.at[2], recv_sems.at[2], zc)

    for copy in middle_copies:
        copy.wait_recv()
    loads[4].wait()
    coarse_layer(middle_bufs, second_w, deep_bufs)
    deep_copies = exchange(*deep_bufs, send_sems.at[3], recv_sems.at[3], zc)

    for copy in skip_copies:
        copy.wait_recv()
    fine_half = half_mask((size_y + 2) * zc)

    @pl.loop(0, size_x + 2)
    def _(x):
        sf[x] = flat(sp[x])
        down, upper = shifted(sf[x], spread(s_below[x], zc), spread(s_above[x], zc), zc)
        se[x] = jnp.where(fine_half, upper, down)

    loads[5].wait()

    @pl.loop(0, xc)
    def _(x):
        acc[x] = fine_conv(sf, se, skip_w, 2 * x, 2, size_y, zc)

    for copy in deep_copies:
        copy.wait_recv()
    coarse_rows = (yc + 2) * zc
    _, coarse_end = masks(coarse_rows, zc)

    def interleaved(value):
        even = value[:, 128:].reshape(yc + 2, zc, 128)[: yc + 1]
        odd = value[:, :128].reshape(yc + 2, zc, 128)[1:]
        return jnp.stack([even, odd], axis=1).reshape((size_y + 2) * zc, 128)

    for x in range(size_x + 2):
        source, a = (x + 1) // 2, (x + 1) % 2
        kernel = jnp.concatenate([up_ref[2 * a], up_ref[2 * a + 1]], axis=0)
        edge_rows = jnp.where(
            coarse_end, spread(d_above[source], zc), spread(d_below[source], zc)
        )
        plane = interleaved(rounded(dot(flat(d_body[source]).astype(BF16), kernel)).astype(F32))
        edge = interleaved(rounded(dot(edge_rows.astype(BF16), kernel)).astype(F32))
        down, upper = shifted(plane, edge, edge, zc)
        up[x] = plane
        ue[x] = jnp.where(fine_half, upper, down)

    @pl.loop(0, xc)
    def _(x):
        joined = rounded(acc[x] + fine_conv(up, ue, wide_w, 2 * x, 2, size_y, zc))
        result = dot(head_ref[...], joined)
        out_ref[2 * x] = result[:, : yc * zc]
        out_ref[2 * x + 1] = result[:, yc * zc :]

    for copy in cell_copies + coarse_copies + skip_copies + middle_copies + deep_copies:
        copy.wait_send()


def local(
    displacement, lift_weight, encode_weight, downward_weight, middle_first, middle_second,
    up_weight, decode_weight, head_weight,
):
    comps, size_x, size_y, size_z = displacement.shape
    c1, c2 = encode_weight.shape[1], middle_first.shape[1]
    xc, yc, zc = size_x // 2, size_y // 2, size_z // 2
    rows_y = size_y + 8

    cells = jnp.transpose(displacement, (1, 2, 3, 0)).reshape(size_x, size_y, -1)
    cells = jnp.pad(cells, ((0, 0), (0, 0), (0, 128 - cells.shape[-1])))
    lift = jnp.pad(lift_weight, ((0, 0), (0, 0), (0, 128 - comps)))
    up_w = up_weight.reshape(4, 2 * c1, c2)
    head = jnp.einsum("pq,ki->pkqi", jnp.eye(4, dtype=BF16), head_weight).reshape(
        4 * comps, 4 * c1
    )
    head = jnp.pad(head, ((0, 16 - 4 * comps), (0, 0)))

    def coarse_set():
        return [
            pltpu.VMEM((xc + 2, yc + 2, zc, 128), BF16),
            pltpu.VMEM((xc + 2, yc + 2, 1, 128), F32),
            pltpu.VMEM((xc + 2, yc + 2, 1, 128), F32),
            pltpu.VMEM((xc, yc, 1, 128), F32),
            pltpu.VMEM((xc, yc, 1, 128), F32),
        ]

    fine = pltpu.VMEM((size_x + 2, (size_y + 2) * zc, 128), F32)
    first = pltpu.VMEM((size_x + 2, rows_y * zc, 128), F32)
    vmem, anywhere = pl.BlockSpec(memory_space=pltpu.VMEM), pl.BlockSpec(memory_space=pltpu.HBM)
    result = pl.pallas_call(
        functools.partial(unet, (comps, size_x, size_y, size_z, rows_y)),
        out_shape=jax.ShapeDtypeStruct((size_x, 16, yc * zc), F32),
        in_specs=[vmem, vmem] + [anywhere] * 6 + [vmem],
        out_specs=vmem,
        scratch_shapes=[
            pltpu.VMEM((size_x + 4, size_y // RIM + 2, RIM, 128), BF16),
            pltpu.VMEM((3, size_y // RIM + 2, RIM, 128), BF16),
            pltpu.VMEM((3, size_y // RIM + 2, RIM, 128), BF16),
            pltpu.VMEM((size_y // RIM, RIM, 128), BF16),
            pltpu.VMEM((size_y // RIM, RIM, 128), BF16),
            pltpu.VMEM((size_x + 4, size_y + 2 * RIM, 128), F32),
            pltpu.VMEM(((size_x + 2) * rows_y, 640), F32),
            pltpu.VMEM(((size_x + 2) * rows_y, 640), BF16),
            pltpu.VMEM((zc + 1, (size_x + 2) * rows_y, 128), F32),
            first, first,
            pltpu.VMEM((size_x + 2, size_y + 2, zc, 128), BF16),
            fine, fine, fine, fine,
            pltpu.VMEM((xc, 2 * yc * zc, 4 * c1), F32),
            pltpu.VMEM((size_x + 2, size_y + 2, 1, 128), F32),
            pltpu.VMEM((size_x + 2, size_y + 2, 1, 128), F32),
            pltpu.VMEM((size_x, size_y, 1, 128), F32),
            pltpu.VMEM((size_x, size_y, 1, 128), F32),
            coarse_set(), coarse_set(), coarse_set(),
            pltpu.VMEM((xc + 2, (yc + 2) * zc, 128), F32),
            pltpu.VMEM((xc + 2, (yc + 2) * zc, 128), F32),
            pltpu.VMEM((xc + 2, (yc + 2) * zc, 128), F32),
            pltpu.VMEM(encode_weight.shape, BF16),
            pltpu.VMEM(downward_weight.shape, BF16),
            pltpu.VMEM(middle_first.shape, BF16),
            pltpu.VMEM(middle_second.shape, BF16),
            pltpu.VMEM(up_w.shape, BF16),
            pltpu.VMEM(decode_weight.shape, BF16),
            pltpu.VMEM((12, 4 * c1, 4 * c1), BF16),
            pltpu.VMEM((12, 4 * c1, 4 * c1), BF16),
            pltpu.VMEM((12, 4 * c1, 4 * c1), BF16),
            pltpu.SemaphoreType.DMA((6,)),
            pltpu.SemaphoreType.DMA((5, len(DIRS))),
            pltpu.SemaphoreType.DMA((5, len(DIRS))),
        ],
        compiler_params=pltpu.CompilerParams(
            collective_id=0, has_side_effects=True, vmem_limit_bytes=63 * 2**20
        ),
    )(
        cells, lift, encode_weight, downward_weight, middle_first, middle_second, up_w,
        decode_weight, head,
    )
    head_out = result[:, : 4 * comps].reshape(size_x, 2, 2, comps, yc, zc)
    head_out = jnp.transpose(head_out, (3, 0, 4, 1, 5, 2)).reshape(displacement.shape)
    return displacement.astype(F32) + head_out


def solution(mesh):
    placed = (P(None, "gx", "gy", "gz"), P(), P(), P(), P(), P(), P(), P(), P())
    return jax.shard_map(
        local, mesh=mesh, in_specs=placed, out_specs=P(None, "gx", "gy", "gz"), check_vma=False
    )
```

```python
import functools

import jax
import jax.numpy as jnp
from jax import lax
from jax.experimental import pallas as pl
from jax.experimental.pallas import tpu as pltpu
from jax.sharding import PartitionSpec as P

AXES = ("gx", "gy", "gz")
MESH = pl.DeviceIdType.MESH
NT = (((1,), (1,)), ((), ()))
DIRS = [
    (dx, dy, dz) for dx in (-1, 0, 1) for dy in (-1, 0, 1) for dz in (-1, 0, 1)
    if (dx, dy, dz) != (0, 0, 0)
]
F32, BF16 = jnp.float32, jnp.bfloat16
RIM = 8


def leaky(value):
    return jnp.maximum(value, 0.1 * value)


def rounded(value):
    return leaky(value).astype(BF16)


def dot(rows, weight):
    return lax.dot_general(rows, weight, NT, preferred_element_type=F32)


def neighbour(direction):
    return tuple(
        lax.rem(lax.axis_index(axis) + lax.axis_size(axis) + step, lax.axis_size(axis))
        for axis, step in zip(AXES, direction)
    )


def exchange(body, below, above, first, last, sends, recvs, zc):
    size_x, size_y = body.shape[0] - 2, body.shape[1] - 2
    copies = []
    for number, (dx, dy, dz) in enumerate(DIRS):
        def span(step, size, offset):
            if step == 0:
                return (offset, size, 1)
            return (offset + size - 1, 1, 0) if step > 0 else (offset, 1, size + 1)

        if dz == 0:
            sx, nx, tx = span(dx, size_x, 1)
            sy, ny, ty = span(dy, size_y, 1)
            src = body.at[pl.ds(sx, nx), pl.ds(sy, ny)]
            dst = body.at[pl.ds(tx, nx), pl.ds(ty, ny)]
        else:
            sx, nx, tx = span(dx, size_x, 0)
            sy, ny, ty = span(dy, size_y, 0)
            src = (last if dz > 0 else first).at[pl.ds(sx, nx), pl.ds(sy, ny)]
            dst = (below if dz > 0 else above).at[pl.ds(tx, nx), pl.ds(ty, ny)]
        copies.append(
            pltpu.make_async_remote_copy(
                src_ref=src, dst_ref=dst, send_sem=sends.at[number], recv_sem=recvs.at[number],
                device_id=neighbour((dx, dy, dz)), device_id_type=MESH,
            )
        )
    return copies


def launch(copies):
    for copy in copies:
        copy.start()


def send_cells(block, before, after, first, last, sends, recvs):
    size_x, size_y = block.shape[0] - 4, block.shape[1] - 2
    copies = []
    for number, (dx, dy, dz) in enumerate(DIRS):
        sx, nx, tx = {0: (2, size_x, 2), 1: (size_x, 2, 0), -1: (2, 2, size_x + 2)}[dx]
        sy, ny, ty = {0: (0, size_y, 1), 1: (size_y - 1, 1, 0), -1: (0, 1, size_y + 1)}[dy]
        if dz == 0:
            src = block.at[pl.ds(sx, nx), pl.ds(sy + 1, ny)]
            dst = block.at[pl.ds(tx, nx), pl.ds(ty, ny)]
        else:
            src = (last if dz > 0 else first).at[pl.ds(sy, ny)]
            dst = (before if dz > 0 else after).at[1 - dx, pl.ds(ty, ny)]
        copies.append(
            pltpu.make_async_remote_copy(
                src_ref=src, dst_ref=dst, send_sem=sends.at[number], recv_sem=recvs.at[number],
                device_id=neighbour((dx, dy, dz)), device_id_type=MESH,
            )
        )
    for copy in copies:
        copy.start()
    return copies


def build_fine(raw, wide, lo, hi):
    out = raw.shape[1]
    blank = jnp.zeros((2 * out, wide.shape[2]), BF16)
    zero = jnp.zeros((out, hi - lo), BF16)
    for a in range(3):
        wide[4 * a, 2 * out :, :] = blank
        wide[4 * a + 3, : 2 * out, :] = blank
        for b in range(3):
            taps = [raw[9 * a + 3 * b + c][:, lo:hi] for c in range(3)]
            low = jnp.concatenate([taps[1], taps[2], zero, taps[0]], axis=1)
            high = jnp.concatenate([taps[0], taps[1], taps[2], zero], axis=1)
            pair = jnp.concatenate([low, high], axis=0)
            wide[4 * a + b, : 2 * out, :] = pair
            wide[4 * a + b + 1, 2 * out :, :] = pair


def masks(rows, zc):
    row = lax.rem(lax.broadcasted_iota(jnp.int32, (rows, 128), 0), zc)
    return row == 0, row == zc - 1


def half_mask(rows):
    return lax.broadcasted_iota(jnp.int32, (rows, 128), 1) < 64


def flat(plane):
    return plane.astype(F32).reshape(plane.shape[0] * plane.shape[1], 128)


def spread(edge, zc):
    return jnp.broadcast_to(edge, (edge.shape[0], zc, 128)).reshape(edge.shape[0] * zc, 128)


def shifted(plane, below, above, zc):
    rows = plane.shape[0]
    start, end = masks(rows, zc)
    down = jnp.where(start, below, pltpu.roll(plane, 1, 0))
    up = jnp.where(end, above, pltpu.roll(plane, rows - 1, 0))
    return down, up


def fine_conv(plane, twin, weight, x0, group, size_y, zc):
    summed = None
    pairs = size_y // 2
    for a in range(3):
        parts = []
        for source in (plane, twin):
            halves = [[], []]
            for g in range(group):
                value = source[x0 + g + a, pl.ds(0, (size_y + 2) * zc), :]
                value = value.reshape(pairs + 1, 2, zc, 128)
                halves[0].append(value[:, 0])
                halves[1].append(value[:, 1])
            parts.append(halves)
        for b in range(4):
            cut = [
                jnp.concatenate(
                    [
                        v[b // 2 : b // 2 + pairs].reshape(pairs * zc, 128)
                        for v in halves[b % 2]
                    ],
                    axis=0,
                ).astype(BF16)
                for halves in parts
            ]
            term = dot(jnp.concatenate(cut, axis=1), weight[4 * a + b])
            summed = term if summed is None else summed + term
    return summed


def coarse_conv(body, low, high, weight, zc):
    size_x, rows = body.shape[0] - 2, body.shape[1] - 2 * zc
    summed = None
    for a in range(3):
        for b in range(3):
            lhs = jnp.concatenate(
                [
                    jnp.concatenate(
                        [ref[x + a, pl.ds(b * zc, rows), :] for x in range(size_x)], axis=0
                    ).astype(BF16)
                    for ref in (low, body, high)
                ],
                axis=1,
            )
            tap = 9 * a + 3 * b
            kernel = jnp.concatenate([weight[tap], weight[tap + 1], weight[tap + 2]], axis=1)
            term = dot(lhs, kernel)
            summed = term if summed is None else summed + term
    return summed


def unet(
    sizes,
    cells_ref, lift_ref, encode_hbm, downward_hbm, first_hbm, second_hbm, up_hbm,
    decode_hbm, head_ref,
    out_ref,
    block, before, after, cell_first, cell_last, joint, lhs32, lhs16, chunks, fp, fe, sp, sf, se, up, ue, acc,
    s_below, s_above, s_first, s_last,
    coarse_bufs, middle_bufs, deep_bufs, low, middle, high,
    encode_raw, downward_raw, first_w, second_w, up_ref, decode_raw,
    encode_w, skip_w, wide_w,
    load_sems, send_sems, recv_sems,
):
    comps, size_x, size_y, size_z, rows_y = sizes
    zc, yc, xc = size_z // 2, size_y // 2, size_x // 2
    loads = [
        pltpu.make_async_copy(src, dst, load_sems.at[i])
        for i, (src, dst) in enumerate(
            (
                (encode_hbm, encode_raw), (downward_hbm, downward_raw), (first_hbm, first_w),
                (decode_hbm, decode_raw), (second_hbm, second_w), (up_hbm, up_ref),
            )
        )
    ]
    for load in loads:
        load.start()
    barrier = pltpu.get_barrier_semaphore()
    for direction in DIRS:
        pl.semaphore_signal(barrier, inc=1, device_id=neighbour(direction), device_id_type=MESH)
    width, edge = comps * size_z, 2 * comps
    own_rows = lax.broadcasted_iota(jnp.int32, (size_y, 128), 1)
    rims = [None, None]
    for x in range(size_x):
        value = cells_ref[x].astype(F32)
        block[x + 2, pl.ds(1, size_y // RIM)] = value.reshape(size_y // RIM, RIM, 128).astype(
            BF16
        )
        for side, start in enumerate((0, width - edge)):
            kept = jnp.where((own_rows >= start) & (own_rows < start + edge), value, 0.0)
            shift = (edge * x - start) % 128
            kept = pltpu.roll(kept, shift, 1) if shift else kept
            rims[side] = kept if rims[side] is None else rims[side] + kept
    cell_first[...] = rims[0].reshape(size_y // RIM, RIM, 128).astype(BF16)
    cell_last[...] = rims[1].reshape(size_y // RIM, RIM, 128).astype(BF16)
    pl.semaphore_wait(barrier, len(DIRS))
    cell_copies = send_cells(
        block, before, after, cell_first, cell_last, send_sems.at[4], recv_sems.at[4]
    )

    groups = []
    for g in range(5):
        total = None
        for tap in range(2 * g, min(2 * g + 2, 9)):
            for c in range(3):
                piece = lift_ref[3 * tap + c].astype(F32)
                blank = jnp.zeros((piece.shape[0], 128 - comps), F32)
                piece = jnp.concatenate([piece, blank], axis=1)
                shift = 64 * (tap % 2) + comps * c
                piece = pltpu.roll(piece, shift, 1) if shift else piece
                total = piece if total is None else total + piece
        groups.append(total)
    loads[0].wait()
    build_fine(encode_raw, encode_w, 0, encode_raw.shape[2])
    loads[1].wait()
    downward = [
        jnp.concatenate([downward_raw[4 * a + t] for t in range(4)], axis=1) for a in range(2)
    ]
    for copy in cell_copies:
        copy.wait_recv()

    all_rows = size_y + 2 * RIM
    lane = lax.broadcasted_iota(jnp.int32, (all_rows, 128), 1)

    def turned(value, shift):
        return pltpu.roll(value, shift % 128, 1) if shift % 128 else value

    for x in range(size_x + 4):
        near, place = (
            (0, size_x - 2 + x) if x < 2 else (1, x - 2) if x < size_x + 2
            else (2, x - size_x - 2)
        )
        own = turned(flat(block[x]), edge)
        before_x = turned(flat(before[near]), -edge * place)
        after_x = turned(flat(after[near]), width + edge - edge * place)
        joint[x] = jnp.where(
            lane < edge,
            before_x,
            jnp.where(lane < edge + width, own, jnp.where(lane < width + 2 * edge, after_x, 0.0)),
        )
    half = half_mask(rows_y)
    for x in range(size_x + 2):
        for g in range(5):
            parts = [
                joint[x + tap // 3, pl.ds(RIM - 2 + tap % 3, rows_y), :]
                for tap in range(2 * g, min(2 * g + 2, 9))
            ]
            other = pltpu.roll(parts[1], 64, 1) if len(parts) > 1 else jnp.zeros_like(parts[0])
            lhs32[pl.ds(x * rows_y, rows_y), 128 * g : 128 * g + 128] = jnp.where(
                half, parts[0], other
            )
    lhs16[...] = lhs32[...].astype(BF16)

    for p in range(zc + 1):
        z_lo, z_hi = (2 * p, 2 * p + 1) if p < zc else (size_z, -1)
        kernel = jnp.concatenate(
            [
                jnp.concatenate(
                    [pltpu.roll(v, comps * (z + 1), 1) if z + 1 else v for v in groups], axis=1
                )
                for z in (z_lo, z_hi)
            ],
            axis=0,
        ).astype(BF16)
        chunks[p] = rounded(dot(lhs16[...], kernel)).astype(F32)
    for x in range(size_x + 2):
        span = pl.ds(x * rows_y, rows_y)
        for p in range(zc):
            fp[x, pl.ds(p, rows_y, stride=zc), :] = chunks[p, span, :]
            fe[x, pl.ds(p, rows_y, stride=zc), :] = jnp.where(
                half, chunks[p + 1, span, :], chunks[zc if p == 0 else p - 1, span, :]
            )

    c_body, c_below, c_above, c_first, c_last = coarse_bufs
    m_body, m_below, m_above, m_first, m_last = middle_bufs
    d_body, d_below, d_above, d_first, d_last = deep_bufs

    @pl.loop(0, xc)
    def _(x):
        skip = rounded(fine_conv(fp, fe, encode_w, 2 * x, 2, size_y, zc))
        half_rows = yc * zc
        coarse = None
        for g in range(2):
            part = skip[g * half_rows : (g + 1) * half_rows]
            term = dot(part, downward[g])
            coarse = term if coarse is None else coarse + term
            wide = part.astype(F32)
            plane = jnp.stack(
                [wide[:, :128].reshape(yc, zc, 128), wide[:, 128:].reshape(yc, zc, 128)], axis=1
            ).reshape(size_y, zc, 128)
            sp[2 * x + g + 1, pl.ds(1, size_y)] = plane.astype(BF16)
            s_first[2 * x + g] = plane[:, 0:1, :]
            s_last[2 * x + g] = plane[:, zc - 1 : zc, :]
        coarse = rounded(coarse).astype(F32)
        c_body[x + 1, pl.ds(1, yc)] = coarse.reshape(yc, zc, 128).astype(BF16)
        c_first[x] = coarse.reshape(yc, zc, 128)[:, 0:1, :]
        c_last[x] = coarse.reshape(yc, zc, 128)[:, zc - 1 : zc, :]

    coarse_copies = exchange(*coarse_bufs, send_sems.at[0], recv_sems.at[0], zc)
    launch(coarse_copies)
    skip_copies = exchange(
        sp, s_below, s_above, s_first, s_last, send_sems.at[1], recv_sems.at[1], zc
    )

    launch([c for c, d in zip(skip_copies, DIRS) if d[0] == 0])

    def coarse_layer(bufs, weight, result):
        body, below, above = bufs[:3]
        for x in range(xc + 2):
            middle[x] = flat(body[x])
            down, upper = shifted(middle[x], spread(below[x], zc), spread(above[x], zc), zc)
            low[x] = down
            high[x] = upper
        value = rounded(coarse_conv(middle, low, high, weight, zc)).astype(F32)
        target, _, _, first, last = result
        for x in range(xc):
            part = value[x * yc * zc : (x + 1) * yc * zc]
            target[x + 1, pl.ds(1, yc)] = part.reshape(yc, zc, 128).astype(BF16)
            first[x] = part.reshape(yc, zc, 128)[:, 0:1, :]
            last[x] = part.reshape(yc, zc, 128)[:, zc - 1 : zc, :]

    loads[2].wait()
    loads[3].wait()
    channels = decode_raw.shape[2] // 2
    build_fine(decode_raw, skip_w, 0, channels)
    build_fine(decode_raw, wide_w, channels, 2 * channels)
    for copy in coarse_copies:
        copy.wait_recv()
    coarse_layer(coarse_bufs, first_w, middle_bufs)
    middle_copies = exchange(*middle_bufs, send_sems.at[2], recv_sems.at[2], zc)
    launch(middle_copies)
    launch([c for c, d in zip(skip_copies, DIRS) if d[0] != 0])

    for copy in middle_copies:
        copy.wait_recv()
    loads[4].wait()
    coarse_layer(middle_bufs, second_w, deep_bufs)
    deep_copies = exchange(*deep_bufs, send_sems.at[3], recv_sems.at[3], zc)
    launch(deep_copies)

    for copy in skip_copies:
        copy.wait_recv()
    fine_half = half_mask((size_y + 2) * zc)

    @pl.loop(0, size_x + 2)
    def _(x):
        sf[x] = flat(sp[x])
        down, upper = shifted(sf[x], spread(s_below[x], zc), spread(s_above[x], zc), zc)
        se[x] = jnp.where(fine_half, upper, down)

    loads[5].wait()

    @pl.loop(0, xc)
    def _(x):
        acc[x] = fine_conv(sf, se, skip_w, 2 * x, 2, size_y, zc)

    for copy in deep_copies:
        copy.wait_recv()
    coarse_rows = (yc + 2) * zc
    _, coarse_end = masks(coarse_rows, zc)

    def interleaved(value):
        even = value[:, 128:].reshape(yc + 2, zc, 128)[: yc + 1]
        odd = value[:, :128].reshape(yc + 2, zc, 128)[1:]
        return jnp.stack([even, odd], axis=1).reshape((size_y + 2) * zc, 128)

    for x in range(size_x + 2):
        source, a = (x + 1) // 2, (x + 1) % 2
        kernel = jnp.concatenate([up_ref[2 * a], up_ref[2 * a + 1]], axis=0)
        edge_rows = jnp.where(
            coarse_end, spread(d_above[source], zc), spread(d_below[source], zc)
        )
        plane = interleaved(rounded(dot(flat(d_body[source]).astype(BF16), kernel)).astype(F32))
        edge = interleaved(rounded(dot(edge_rows.astype(BF16), kernel)).astype(F32))
        down, upper = shifted(plane, edge, edge, zc)
        up[x] = plane
        ue[x] = jnp.where(fine_half, upper, down)

    @pl.loop(0, xc)
    def _(x):
        joined = rounded(acc[x] + fine_conv(up, ue, wide_w, 2 * x, 2, size_y, zc))
        result = dot(head_ref[...], joined)
        out_ref[2 * x] = result[:, : yc * zc]
        out_ref[2 * x + 1] = result[:, yc * zc :]

    for copy in cell_copies + coarse_copies + skip_copies + middle_copies + deep_copies:
        copy.wait_send()


def local(
    displacement, lift_weight, encode_weight, downward_weight, middle_first, middle_second,
    up_weight, decode_weight, head_weight,
):
    comps, size_x, size_y, size_z = displacement.shape
    c1, c2 = encode_weight.shape[1], middle_first.shape[1]
    xc, yc, zc = size_x // 2, size_y // 2, size_z // 2
    rows_y = size_y + 8

    cells = jnp.transpose(displacement, (1, 2, 3, 0)).reshape(size_x, size_y, -1)
    cells = jnp.pad(cells, ((0, 0), (0, 0), (0, 128 - cells.shape[-1])))
    up_w = up_weight.reshape(4, 2 * c1, c2)
    head = jnp.einsum("pq,ki->pkqi", jnp.eye(4, dtype=BF16), head_weight).reshape(
        4 * comps, 4 * c1
    )
    head = jnp.pad(head, ((0, 16 - 4 * comps), (0, 0)))

    def coarse_set():
        return [
            pltpu.VMEM((xc + 2, yc + 2, zc, 128), BF16),
            pltpu.VMEM((xc + 2, yc + 2, 1, 128), F32),
            pltpu.VMEM((xc + 2, yc + 2, 1, 128), F32),
            pltpu.VMEM((xc, yc, 1, 128), F32),
            pltpu.VMEM((xc, yc, 1, 128), F32),
        ]

    fine = pltpu.VMEM((size_x + 2, (size_y + 2) * zc, 128), F32)
    first = pltpu.VMEM((size_x + 2, rows_y * zc, 128), F32)
    vmem, anywhere = pl.BlockSpec(memory_space=pltpu.VMEM), pl.BlockSpec(memory_space=pltpu.HBM)
    result = pl.pallas_call(
        functools.partial(unet, (comps, size_x, size_y, size_z, rows_y)),
        out_shape=jax.ShapeDtypeStruct((size_x, 16, yc * zc), F32),
        in_specs=[vmem, vmem] + [anywhere] * 6 + [vmem],
        out_specs=vmem,
        scratch_shapes=[
            pltpu.VMEM((size_x + 4, size_y // RIM + 2, RIM, 128), BF16),
            pltpu.VMEM((3, size_y // RIM + 2, RIM, 128), BF16),
            pltpu.VMEM((3, size_y // RIM + 2, RIM, 128), BF16),
            pltpu.VMEM((size_y // RIM, RIM, 128), BF16),
            pltpu.VMEM((size_y // RIM, RIM, 128), BF16),
            pltpu.VMEM((size_x + 4, size_y + 2 * RIM, 128), F32),
            pltpu.VMEM(((size_x + 2) * rows_y, 640), F32),
            pltpu.VMEM(((size_x + 2) * rows_y, 640), BF16),
            pltpu.VMEM((zc + 1, (size_x + 2) * rows_y, 128), F32),
            first, first,
            pltpu.VMEM((size_x + 2, size_y + 2, zc, 128), BF16),
            fine, fine, fine, fine,
            pltpu.VMEM((xc, 2 * yc * zc, 4 * c1), F32),
            pltpu.VMEM((size_x + 2, size_y + 2, 1, 128), F32),
            pltpu.VMEM((size_x + 2, size_y + 2, 1, 128), F32),
            pltpu.VMEM((size_x, size_y, 1, 128), F32),
            pltpu.VMEM((size_x, size_y, 1, 128), F32),
            coarse_set(), coarse_set(), coarse_set(),
            pltpu.VMEM((xc + 2, (yc + 2) * zc, 128), F32),
            pltpu.VMEM((xc + 2, (yc + 2) * zc, 128), F32),
            pltpu.VMEM((xc + 2, (yc + 2) * zc, 128), F32),
            pltpu.VMEM(encode_weight.shape, BF16),
            pltpu.VMEM(downward_weight.shape, BF16),
            pltpu.VMEM(middle_first.shape, BF16),
            pltpu.VMEM(middle_second.shape, BF16),
            pltpu.VMEM(up_w.shape, BF16),
            pltpu.VMEM(decode_weight.shape, BF16),
            pltpu.VMEM((12, 4 * c1, 4 * c1), BF16),
            pltpu.VMEM((12, 4 * c1, 4 * c1), BF16),
            pltpu.VMEM((12, 4 * c1, 4 * c1), BF16),
            pltpu.SemaphoreType.DMA((6,)),
            pltpu.SemaphoreType.DMA((5, len(DIRS))),
            pltpu.SemaphoreType.DMA((5, len(DIRS))),
        ],
        compiler_params=pltpu.CompilerParams(
            collective_id=0, has_side_effects=True, vmem_limit_bytes=63 * 2**20
        ),
    )(
        cells, lift_weight, encode_weight, downward_weight, middle_first, middle_second, up_w,
        decode_weight, head,
    )
    head_out = result[:, : 4 * comps].reshape(size_x, 2, 2, comps, yc, zc)
    head_out = jnp.transpose(head_out, (3, 0, 4, 1, 5, 2)).reshape(displacement.shape)
    return displacement.astype(F32) + head_out


def solution(mesh):
    placed = (P(None, "gx", "gy", "gz"), P(), P(), P(), P(), P(), P(), P(), P())
    return jax.shard_map(
        local, mesh=mesh, in_specs=placed, out_specs=P(None, "gx", "gy", "gz"), check_vma=False
    )
```
